32 devices in a mesh: tm: 4 (over x, core), cell: 8 (over z, y).
Axes of the slice: x: 2, y: 2, z: 4, core: 2. Of those that a mesh axis runs over, the one named last changes fastest.
Arguments:
- coords: float32 [4, 64, 4096], P('tm', None, 'cell'), may hold values from -8 to 8
- potentials: float32 [4, 4096], P('tm', 'cell'), may hold values from -6 to 202
Outputs:
- beliefs: float32 [4, 4096], P('tm', 'cell')
The draws below stay inside these ranges and needn't reach their ends.
All inputs are finite; a program needn't handle non-finite values.
Results may differ from the reference program's by a relative error of at most 0.00011.
Values sent between devices are 32-bit elements; how exact they have to be, the bound alone decides.
A program may use at most 64 MiB of HBM per device.

```python
import math
import jax
import jax.numpy as jnp
from jax import lax

DIM = 64
TIMES = 4
CELLS = 4096


def draw_coords(key, part):
    base = jax.random.normal(jax.random.fold_in(key, 71), (TIMES, DIM, CELLS), jnp.float32)
    return jnp.clip(base * 0.25, -8.0, 8.0)


def draw_potentials(key, part):
    own_key = jax.random.fold_in(key, 72)
    return jnp.clip(jax.random.normal(own_key, (TIMES, CELLS), jnp.float32), -6.0, 6.0)


def setup_inputs(seed: int = 0) -> dict:
    arg_keys = jax.random.split(jax.random.key(seed), 3)
    coords = draw_coords(jax.random.fold_in(arg_keys[2], 71), 0)
    potentials = draw_potentials(jax.random.fold_in(arg_keys[2], 71), 0)
    return dict(coords=coords, potentials=potentials)


EPS = 1.0


def message(sources, belief, targets):
    src_sq = jnp.sum(sources * sources, axis=0)
    width = min(512, targets.shape[1])
    blocks = targets.reshape(targets.shape[0], targets.shape[1] // width, width).transpose(1, 0, 2)

    def one_block(block):
        cross = lax.dot_general(sources, block, (((0,), (0,)), ((), ())), precision=lax.Precision.HIGHEST, preferred_element_type=jnp.float32)
        dist = (src_sq[:, None] + jnp.sum(block * block, axis=0)[None, :]) - 2.0 * cross
        score = belief[:, None] - dist / EPS
        return jax.nn.logsumexp(score, axis=0)

    return lax.map(one_block, blocks).reshape(-1)


def reference(coords, potentials):
    offset = math.log(CELLS)
    rows = [potentials[0]]
    for step in range(TIMES - 1):
        result = message(coords[step], rows[-1], coords[step + 1])
        rows.append(result - offset + potentials[step + 1])
    return jnp.stack(rows, axis=0)
```

```python
import functools
import math

import jax
import jax.numpy as jnp
from jax import lax
from jax.experimental import pallas as pl
from jax.experimental.pallas import tpu as pltpu
from jax.sharding import PartitionSpec as P

EPS = 1.0
LOG2E = math.log2(math.e) / EPS
LN2 = math.log(2.0) * EPS
CHUNKS = 4
MESH = pl.DeviceIdType.MESH


def kernel(
    n,
    times,
    coords_hbm,
    pot_hbm,
    out_ref,
    own,
    pot,
    block,
    beliefs,
    sent,
    split_y,
    split_x,
    score,
    x_sq,
    top,
    total,
    load_sem,
    coord_send,
    relay_send,
    coord_recv,
    belief_send,
    belief_recv,
):
    dim, local = own.shape
    half = n // 2
    rows = dim // CHUNKS
    t = lax.axis_index("tm")
    cell = lax.axis_index("cell")
    me = jnp.where(cell % 2 == 0, cell // 2, n - 1 - cell // 2)

    def cell_of(pos):
        return jnp.where(pos < half, 2 * pos, 2 * (n - 1 - pos) + 1)

    def at(group, shift):
        return (group, cell_of(lax.rem(me + shift + n, n)))

    load_own = pltpu.make_async_copy(coords_hbm.at[0], own, load_sem.at[0])
    load_pot = pltpu.make_async_copy(pot_hbm, pot, load_sem.at[1])
    load_own.start()
    load_pot.start()

    barrier = pltpu.get_barrier_semaphore()

    @pl.when(t > 0)
    def _():
        for shift in (1, n - 1):
            pl.semaphore_signal(barrier, inc=1, device_id=at(t, shift), device_id_type=MESH)

        @pl.loop(0, n)
        def _(shift):
            pl.semaphore_signal(barrier, inc=1, device_id=at(t - 1, shift), device_id_type=MESH)

    pl.semaphore_wait(barrier, jnp.where(t < times - 1, n, 0) + jnp.where(t > 0, 2, 0))

    def first_copy(kind, chunk):
        shift = (1, n - 1, 0)[kind]
        return pltpu.make_async_remote_copy(
            src_ref=coords_hbm.at[0, pl.ds(chunk * rows, rows)],
            dst_ref=block.at[shift, pl.ds(chunk * rows, rows)],
            send_sem=coord_send.at[kind, chunk],
            recv_sem=coord_recv.at[shift, chunk],
            device_id=at(t + 1, shift),
            device_id_type=MESH,
        )

    def belief_copy(source, shift):
        return pltpu.make_async_remote_copy(
            src_ref=source,
            dst_ref=beliefs.at[shift],
            send_sem=belief_send.at[shift],
            recv_sem=belief_recv.at[shift],
            device_id=at(t + 1, shift),
            device_id_type=MESH,
        )

    def relay(source_slot, target_slot, chunk, shift):
        return pltpu.make_async_remote_copy(
            src_ref=block.at[source_slot, pl.ds(chunk * rows, rows)],
            dst_ref=block.at[target_slot, pl.ds(chunk * rows, rows)],
            send_sem=relay_send.at[target_slot, chunk],
            recv_sem=coord_recv.at[target_slot, chunk],
            device_id=at(t, shift),
            device_id_type=MESH,
        )

    @pl.when(t < times - 1)
    def _():
        for chunk in range(CHUNKS):
            first_copy(0, chunk).start()
            first_copy(1, chunk).start()
        for chunk in range(CHUNKS):
            first_copy(2, chunk).start()

    load_pot.wait()

    @pl.when(t == 0)
    def _():
        @pl.loop(0, n)
        def _(shift):
            belief_copy(pot, shift).start()

    def forward(dist):
        right_in, left_in = dist, n - dist
        last = dist + 1 == half
        for chunk in range(CHUNKS):
            relay(right_in, right_in, chunk, 1).wait_recv()
            if chunk < CHUNKS // 2:
                relay(right_in, dist + 1, chunk, 1).start()
            else:

                @pl.when(jnp.logical_not(last))
                def _():
                    relay(right_in, dist + 1, chunk, 1).start()

            relay(left_in, left_in, chunk, 1).wait_recv()
            if chunk >= CHUNKS // 2:
                relay(left_in, n - dist - 1, chunk, n - 1).start()
            else:

                @pl.when(jnp.logical_not(last))
                def _():
                    relay(left_in, n - dist - 1, chunk, n - 1).start()

    def arrive(slot):
        for chunk in range(CHUNKS):
            relay(slot, slot, chunk, 1).wait_recv()

    def make_scores(slot):
        x = block[slot]
        hi = x.astype(jnp.bfloat16)
        lo = (x - hi.astype(jnp.float32)).astype(jnp.bfloat16)
        split_x[pl.ds(0, dim)] = hi
        split_x[pl.ds(dim, dim)] = lo
        split_x[pl.ds(2 * dim, dim)] = hi
        split_x[pl.ds(3 * dim, dim)] = lo
        x_sq[slot] = jnp.sum(x * x, axis=0, keepdims=True)
        score[slot] = lax.dot_general(
            split_y[...],
            split_x[...],
            (((1,), (0,)), ((), ())),
            preferred_element_type=jnp.float32,
        )

    tile = 32

    def fold(slot):
        row = LOG2E * (beliefs[slot] - x_sq[slot])

        @pl.loop(0, local // tile, unroll=4)
        def _(step):
            here = pl.ds(pl.multiple_of(step * tile, tile), tile)
            parts = [
                score[slot, here, pl.ds(k, 128)] + row[:, k : k + 128]
                for k in range(0, local, 128)
            ]
            old = top[here]
            new = old
            for part in parts:
                new = jnp.maximum(new, part)
            acc = total[here] * jnp.exp2(old - new)
            for part in parts:
                acc = acc + jnp.exp2(part - new)
            top[here] = new
            total[here] = acc

    def slot_of(step):
        near = (step + 1) // 2
        return jnp.where(step % 2 == 1, near, lax.rem(n - near, n))

    @pl.when(t > 0)
    def _():
        load_own.wait()
        turned = (own[...] * (2.0 * LOG2E)).T
        hi = turned.astype(jnp.bfloat16)
        lo = (turned - hi.astype(jnp.float32)).astype(jnp.bfloat16)
        split_y[:, 0:dim] = hi
        split_y[:, dim : 2 * dim] = hi
        split_y[:, 2 * dim : 3 * dim] = lo
        split_y[:, 3 * dim : 4 * dim] = lo
        top[...] = jnp.full_like(top, -1e30)
        total[...] = jnp.zeros_like(total)

        def consume(slot):
            make_scores(slot)

            @pl.when(t == 1)
            def _():
                belief_copy(pot, slot).wait_recv()
                fold(slot)

        @pl.loop(1, half)
        def _(dist):
            forward(dist)

            @pl.when(dist == 1)
            def _():
                arrive(0)
                consume(0)

            @pl.when(dist > 1)
            def _():
                @pl.loop(2 * dist - 3, 2 * dist - 1)
                def _(step):
                    consume(slot_of(step))

        @pl.loop(n - 3, n)
        def _(step):
            @pl.when(step == n - 1)
            def _():
                arrive(half)

            consume(slot_of(step))

        @pl.when(t > 1)
        def _():
            @pl.loop(0, n)
            def _(step):
                slot = slot_of(step)
                belief_copy(pot, slot).wait_recv()
                fold(slot)

        tops = top[...].T
        peak = jnp.max(tops, axis=0, keepdims=True)
        mass = jnp.sum(total[...].T * jnp.exp2(tops - peak), axis=0, keepdims=True)
        y = own[...]
        y_sq = jnp.sum(y * y, axis=0, keepdims=True)
        sent[...] = (
            LN2 * (peak + jnp.log2(mass)) - y_sq / EPS - math.log(n * local) + pot[...]
        )

        @pl.when(t < times - 1)
        def _():
            @pl.loop(0, n)
            def _(shift):
                belief_copy(sent, shift).start()

        out_ref[...] = sent[...]

        @pl.loop(1, half)
        def _(dist):
            last = dist + 1 == half
            for chunk in range(CHUNKS):
                if chunk < CHUNKS // 2:
                    relay(dist, dist + 1, chunk, 1).wait_send()
                else:

                    @pl.when(jnp.logical_not(last))
                    def _():
                        relay(dist, dist + 1, chunk, 1).wait_send()

                if chunk >= CHUNKS // 2:
                    relay(n - dist, n - dist - 1, chunk, n - 1).wait_send()
                else:

                    @pl.when(jnp.logical_not(last))
                    def _():
                        relay(n - dist, n - dist - 1, chunk, n - 1).wait_send()

    @pl.when(t == 0)
    def _():
        load_own.wait()
        out_ref[...] = pot[...]

    @pl.when(t < times - 1)
    def _():
        for chunk in range(CHUNKS):
            for kind in range(3):
                first_copy(kind, chunk).wait_send()

        @pl.loop(0, n)
        def _(shift):
            belief_copy(sent, shift).wait_send()


def body(n, times, coords, potentials):
    _, dim, local = coords.shape
    f32, bf16 = jnp.float32, jnp.bfloat16
    dma = pltpu.SemaphoreType.DMA
    return pl.pallas_call(
        functools.partial(kernel, n, times),
        out_shape=jax.ShapeDtypeStruct((1, local), f32),
        in_specs=[pl.BlockSpec(memory_space=pl.ANY)] * 2,
        out_specs=pl.BlockSpec(memory_space=pltpu.VMEM),
        scratch_shapes=[
            pltpu.VMEM((dim, local), f32),
            pltpu.VMEM((1, local), f32),
            pltpu.VMEM((n, dim, local), f32),
            pltpu.VMEM((n, 1, local), f32),
            pltpu.VMEM((1, local), f32),
            pltpu.VMEM((local, 4 * dim), bf16),
            pltpu.VMEM((4 * dim, local), bf16),
            pltpu.VMEM((n, local, local), f32),
            pltpu.VMEM((n, 1, local), f32),
            pltpu.VMEM((local, 128), f32),
            pltpu.VMEM((local, 128), f32),
            dma((2,)),
            dma((3, CHUNKS)),
            dma((n, CHUNKS)),
            dma((n, CHUNKS)),
            dma((n,)),
            dma((n,)),
        ],
        compiler_params=pltpu.CompilerParams(
            collective_id=0, has_side_effects=True, vmem_limit_bytes=60 * 1024 * 1024
        ),
        name="sweep",
    )(coords, potentials)


def solution(mesh):
    return jax.shard_map(
        functools.partial(body, mesh.shape["cell"], mesh.shape["tm"]),
        mesh=mesh,
        in_specs=(P("tm", None, "cell"), P("tm", "cell")),
        out_specs=P("tm", "cell"),
        check_vma=False,
    )
```

```python
import functools
import math

import jax
import jax.numpy as jnp
from jax import lax
from jax.experimental import pallas as pl
from jax.experimental.pallas import tpu as pltpu
from jax.sharding import PartitionSpec as P

EPS = 1.0
LOG2E = math.log2(math.e) / EPS
LN2 = math.log(2.0) * EPS
CHUNKS = 4
MESH = pl.DeviceIdType.MESH


def kernel(
    n,
    times,
    coords_hbm,
    pot_hbm,
    out_ref,
    own,
    pot,
    block,
    beliefs,
    sent,
    split_y,
    split_x,
    score,
    x_sq,
    top,
    total,
    load_sem,
    coord_send,
    relay_send,
    coord_recv,
    belief_send,
    belief_relay,
    belief_recv,
    ready,
):
    dim, local = own.shape
    half = n // 2
    rows = dim // CHUNKS
    t = lax.axis_index("tm")
    cell = lax.axis_index("cell")
    me = jnp.where(cell % 2 == 0, cell // 2, n - 1 - cell // 2)

    def cell_of(pos):
        return jnp.where(pos < half, 2 * pos, 2 * (n - 1 - pos) + 1)

    def at(group, shift):
        return (group, cell_of(lax.rem(me + shift + n, n)))

    barrier = pltpu.get_barrier_semaphore()

    @pl.when(t > 0)
    def _():
        for shift in (0, 1, n - 1):
            pl.semaphore_signal(barrier, inc=1, device_id=at(t - 1, shift), device_id_type=MESH)
        for shift in (1, n - 1):
            pl.semaphore_signal(barrier, inc=1, device_id=at(t, shift), device_id_type=MESH)

    load_own = pltpu.make_async_copy(coords_hbm.at[0], own, load_sem.at[0])
    load_pot = pltpu.make_async_copy(pot_hbm, pot, load_sem.at[1])
    load_own.start()
    load_pot.start()
    pl.semaphore_wait(barrier, jnp.where(t < times - 1, 3, 0) + jnp.where(t > 0, 2, 0))

    def first_copy(kind, chunk):
        shift = (1, n - 1, 0)[kind]
        return pltpu.make_async_remote_copy(
            src_ref=coords_hbm.at[0, pl.ds(chunk * rows, rows)],
            dst_ref=block.at[shift, pl.ds(chunk * rows, rows)],
            send_sem=coord_send.at[kind, chunk],
            recv_sem=coord_recv.at[shift, chunk],
            device_id=at(t + 1, shift),
            device_id_type=MESH,
        )

    def first_belief(kind):
        shift = (1, n - 1, 0)[kind]
        return pltpu.make_async_remote_copy(
            src_ref=pot_hbm,
            dst_ref=beliefs.at[shift],
            send_sem=belief_send.at[shift],
            recv_sem=belief_recv.at[shift],
            device_id=at(t + 1, shift),
            device_id_type=MESH,
        )

    def pass_belief(source_slot, target_slot, shift):
        return pltpu.make_async_remote_copy(
            src_ref=beliefs.at[source_slot],
            dst_ref=beliefs.at[target_slot],
            send_sem=belief_relay.at[target_slot],
            recv_sem=belief_recv.at[target_slot],
            device_id=at(t, shift),
            device_id_type=MESH,
        )

    def belief_copy(source, shift):
        return pltpu.make_async_remote_copy(
            src_ref=source,
            dst_ref=beliefs.at[shift],
            send_sem=belief_send.at[shift],
            recv_sem=belief_recv.at[shift],
            device_id=at(t + 1, shift),
            device_id_type=MESH,
        )

    def relay(source_slot, target_slot, chunk, shift):
        return pltpu.make_async_remote_copy(
            src_ref=block.at[source_slot, pl.ds(chunk * rows, rows)],
            dst_ref=block.at[target_slot, pl.ds(chunk * rows, rows)],
            send_sem=relay_send.at[target_slot, chunk],
            recv_sem=coord_recv.at[target_slot, chunk],
            device_id=at(t, shift),
            device_id_type=MESH,
        )

    @pl.when(t < times - 1)
    def _():
        for chunk in range(CHUNKS):
            first_copy(0, chunk).start()
            first_copy(1, chunk).start()

            if chunk == 0:

                @pl.when(t == 0)
                def _():
                    for kind in range(3):
                        first_belief(kind).start()

        for chunk in range(CHUNKS):
            first_copy(2, chunk).start()

    def forward(dist, pieces):
        right_in, left_in = dist, n - dist
        last = dist + 1 == half
        for chunk in range(CHUNKS):
            relay(right_in, right_in, chunk, 1).wait_recv()
            if chunk < CHUNKS // 2:
                relay(right_in, dist + 1, chunk, 1).start()
            else:

                @pl.when(jnp.logical_not(last))
                def _():
                    relay(right_in, dist + 1, chunk, 1).start()

            relay(left_in, left_in, chunk, 1).wait_recv()
            if chunk >= CHUNKS // 2:
                relay(left_in, n - dist - 1, chunk, n - 1).start()
            else:

                @pl.when(jnp.logical_not(last))
                def _():
                    relay(left_in, n - dist - 1, chunk, n - 1).start()

            if chunk == 0:

                @pl.when(t == 1)
                def _():
                    pass_belief(right_in, right_in, 1).wait_recv()
                    pass_belief(right_in, dist + 1, 1).start()
                    pass_belief(left_in, left_in, 1).wait_recv()

                    @pl.when(jnp.logical_not(last))
                    def _():
                        pass_belief(left_in, n - dist - 1, n - 1).start()

            if chunk < len(pieces):
                pieces[chunk]()

    def arrive(slot):
        for chunk in range(CHUNKS):
            relay(slot, slot, chunk, 1).wait_recv()

    def make_scores(slot):
        x = block[slot]
        hi = x.astype(jnp.bfloat16)
        lo = (x - hi.astype(jnp.float32)).astype(jnp.bfloat16)
        split_x[pl.ds(0, dim)] = hi
        split_x[pl.ds(dim, dim)] = lo
        split_x[pl.ds(2 * dim, dim)] = hi
        split_x[pl.ds(3 * dim, dim)] = lo
        x_sq[slot] = jnp.sum(x * x, axis=0, keepdims=True)
        score[slot] = lax.dot_general(
            split_y[...],
            split_x[...],
            (((1,), (0,)), ((), ())),
            preferred_element_type=jnp.float32,
        )

    tile = 32

    def fold(slot):
        row = LOG2E * (beliefs[slot] - x_sq[slot])

        @pl.loop(0, local // tile, unroll=4)
        def _(step):
            here = pl.ds(pl.multiple_of(step * tile, tile), tile)
            parts = [
                score[slot, here, pl.ds(k, 128)] + row[:, k : k + 128]
                for k in range(0, local, 128)
            ]
            old = top[here]
            new = old
            for part in parts:
                new = jnp.maximum(new, part)
            acc = total[here] * jnp.exp2(old - new)
            for part in parts:
                acc = acc + jnp.exp2(part - new)
            top[here] = new
            total[here] = acc

    def slot_of(step):
        near = (step + 1) // 2
        return jnp.where(step % 2 == 1, near, lax.rem(n - near, n))

    @pl.when(t > 0)
    def _():
        load_own.wait()
        turned = (own[...] * (2.0 * LOG2E)).T
        hi = turned.astype(jnp.bfloat16)
        lo = (turned - hi.astype(jnp.float32)).astype(jnp.bfloat16)
        split_y[:, 0:dim] = hi
        split_y[:, dim : 2 * dim] = hi
        split_y[:, 2 * dim : 3 * dim] = lo
        split_y[:, 3 * dim : 4 * dim] = lo
        top[...] = jnp.full_like(top, -1e30)
        total[...] = jnp.zeros_like(total)

        def scores_of(slot):
            make_scores(slot)

            @pl.when(t > 1)
            def _():
                pl.semaphore_signal(
                    ready, inc=1, device_id=at(t - 1, n - slot), device_id_type=MESH
                )

        def first_fold(slot):
            @pl.when(t == 1)
            def _():
                fold(slot)

        def await_belief(slot):
            @pl.when(t == 1)
            def _():
                pass_belief(slot, slot, 1).wait_recv()

        forward(1, ())
        arrive(0)
        await_belief(0)
        scores_of(0)
        first_fold(0)

        @pl.loop(2, half)
        def _(dist):
            right, left = dist - 1, n - dist + 1
            forward(
                dist,
                (
                    lambda: scores_of(right),
                    lambda: first_fold(right),
                    lambda: scores_of(left),
                    lambda: first_fold(left),
                ),
            )

        @pl.loop(n - 3, n)
        def _(step):
            slot = slot_of(step)

            @pl.when(step == n - 1)
            def _():
                arrive(half)
                await_belief(half)

            scores_of(slot)
            first_fold(slot)

        @pl.when(t > 1)
        def _():
            @pl.loop(0, n)
            def _(step):
                slot = slot_of(step)
                belief_copy(sent, slot).wait_recv()
                fold(slot)

        tops = top[...].T
        peak = jnp.max(tops, axis=0, keepdims=True)
        mass = jnp.sum(total[...].T * jnp.exp2(tops - peak), axis=0, keepdims=True)
        load_pot.wait()
        y = own[...]
        y_sq = jnp.sum(y * y, axis=0, keepdims=True)
        sent[...] = (
            LN2 * (peak + jnp.log2(mass)) - y_sq / EPS - math.log(n * local) + pot[...]
        )

        @pl.when(t < times - 1)
        def _():
            pl.semaphore_wait(ready, n)

            @pl.loop(0, n)
            def _(step):
                belief_copy(sent, slot_of(n - 1 - step)).start()

        out_ref[...] = sent[...]

        @pl.loop(1, half)
        def _(dist):
            last = dist + 1 == half

            @pl.when(t == 1)
            def _():
                pass_belief(dist, dist + 1, 1).wait_send()

                @pl.when(jnp.logical_not(last))
                def _():
                    pass_belief(n - dist, n - dist - 1, n - 1).wait_send()

            for chunk in range(CHUNKS):
                if chunk < CHUNKS // 2:
                    relay(dist, dist + 1, chunk, 1).wait_send()
                else:

                    @pl.when(jnp.logical_not(last))
                    def _():
                        relay(dist, dist + 1, chunk, 1).wait_send()

                if chunk >= CHUNKS // 2:
                    relay(n - dist, n - dist - 1, chunk, n - 1).wait_send()
                else:

                    @pl.when(jnp.logical_not(last))
                    def _():
                        relay(n - dist, n - dist - 1, chunk, n - 1).wait_send()

    @pl.when(t == 0)
    def _():
        load_own.wait()
        load_pot.wait()
        for kind in range(3):
            first_belief(kind).wait_send()
        out_ref[...] = pot[...]

    @pl.when(t < times - 1)
    def _():
        for chunk in range(CHUNKS):
            for kind in range(3):
                first_copy(kind, chunk).wait_send()

        @pl.when(t > 0)
        def _():
            @pl.loop(0, n)
            def _(shift):
                belief_copy(sent, shift).wait_send()


def body(n, times, coords, potentials):
    _, dim, local = coords.shape
    f32, bf16 = jnp.float32, jnp.bfloat16
    dma = pltpu.SemaphoreType.DMA
    return pl.pallas_call(
        functools.partial(kernel, n, times),
        out_shape=jax.ShapeDtypeStruct((1, local), f32),
        in_specs=[pl.BlockSpec(memory_space=pl.ANY)] * 2,
        out_specs=pl.BlockSpec(memory_space=pltpu.VMEM),
        scratch_shapes=[
            pltpu.VMEM((dim, local), f32),
            pltpu.VMEM((1, local), f32),
            pltpu.VMEM((n, dim, local), f32),
            pltpu.VMEM((n, 1, local), f32),
            pltpu.VMEM((1, local), f32),
            pltpu.VMEM((local, 4 * dim), bf16),
            pltpu.VMEM((4 * dim, local), bf16),
            pltpu.VMEM((n, local, local), f32),
            pltpu.VMEM((n, 1, local), f32),
            pltpu.VMEM((local, 128), f32),
            pltpu.VMEM((local, 128), f32),
            dma((2,)),
            dma((3, CHUNKS)),
            dma((n, CHUNKS)),
            dma((n, CHUNKS)),
            dma((n,)),
            dma((n,)),
            dma((n,)),
            pltpu.SemaphoreType.REGULAR,
        ],
        compiler_params=pltpu.CompilerParams(
            collective_id=0, has_side_effects=True, vmem_limit_bytes=60 * 1024 * 1024
        ),
        name="sweep",
    )(coords, potentials)


def solution(mesh):
    return jax.shard_map(
        functools.partial(body, mesh.shape["cell"], mesh.shape["tm"]),
        mesh=mesh,
        in_specs=(P("tm", None, "cell"), P("tm", "cell")),
        out_specs=P("tm", "cell"),
        check_vma=False,
    )
```

```python
import functools
import math

import jax
import jax.numpy as jnp
from jax import lax
from jax.experimental import pallas as pl
from jax.experimental.pallas import tpu as pltpu
from jax.sharding import PartitionSpec as P

EPS = 1.0
LOG2E = math.log2(math.e) / EPS
LN2 = math.log(2.0) * EPS
CHUNKS = 4
MESH = pl.DeviceIdType.MESH


def kernel(
    n,
    times,
    coords_hbm,
    pot_hbm,
    out_ref,
    own,
    pot,
    block,
    beliefs,
    sent,
    split_y,
    split_x,
    score,
    x_sq,
    top,
    total,
    load_sem,
    coord_send,
    relay_send,
    coord_recv,
    belief_send,
    belief_relay,
    belief_recv,
):
    dim, local = own.shape
    half = n // 2
    rows = dim // CHUNKS
    t = lax.axis_index("tm")
    cell = lax.axis_index("cell")
    me = jnp.where(cell % 2 == 0, cell // 2, n - 1 - cell // 2)

    def cell_of(pos):
        return jnp.where(pos < half, 2 * pos, 2 * (n - 1 - pos) + 1)

    def at(group, shift):
        return (group, cell_of(lax.rem(me + shift + n, n)))

    barrier = pltpu.get_barrier_semaphore()

    @pl.when(t > 0)
    def _():
        for shift in (0, 1, n - 1):
            pl.semaphore_signal(barrier, inc=1, device_id=at(t - 1, shift), device_id_type=MESH)
        for shift in (1, n - 1):
            pl.semaphore_signal(barrier, inc=1, device_id=at(t, shift), device_id_type=MESH)

    load_own = pltpu.make_async_copy(coords_hbm.at[0], own, load_sem.at[0])
    load_pot = pltpu.make_async_copy(pot_hbm, pot, load_sem.at[1])
    load_own.start()
    load_pot.start()
    pl.semaphore_wait(barrier, jnp.where(t < times - 1, 3, 0) + jnp.where(t > 0, 2, 0))

    def first_copy(kind, chunk):
        shift = (1, n - 1, 0)[kind]
        return pltpu.make_async_remote_copy(
            src_ref=coords_hbm.at[0, pl.ds(chunk * rows, rows)],
            dst_ref=block.at[shift, pl.ds(chunk * rows, rows)],
            send_sem=coord_send.at[kind, chunk],
            recv_sem=coord_recv.at[shift, chunk],
            device_id=at(t + 1, shift),
            device_id_type=MESH,
        )

    def first_belief(kind):
        shift = (1, n - 1, 0)[kind]
        return pltpu.make_async_remote_copy(
            src_ref=pot_hbm,
            dst_ref=beliefs.at[shift],
            send_sem=belief_send.at[shift],
            recv_sem=belief_recv.at[shift],
            device_id=at(t + 1, shift),
            device_id_type=MESH,
        )

    def pass_belief(source_slot, target_slot, shift):
        return pltpu.make_async_remote_copy(
            src_ref=beliefs.at[source_slot],
            dst_ref=beliefs.at[target_slot],
            send_sem=belief_relay.at[target_slot],
            recv_sem=belief_recv.at[target_slot],
            device_id=at(t, shift),
            device_id_type=MESH,
        )

    def belief_copy(source, shift):
        return pltpu.make_async_remote_copy(
            src_ref=source,
            dst_ref=beliefs.at[shift],
            send_sem=belief_send.at[shift],
            recv_sem=belief_recv.at[shift],
            device_id=at(t + 1, shift),
            device_id_type=MESH,
        )

    def relay(source_slot, target_slot, chunk, shift):
        return pltpu.make_async_remote_copy(
            src_ref=block.at[source_slot, pl.ds(chunk * rows, rows)],
            dst_ref=block.at[target_slot, pl.ds(chunk * rows, rows)],
            send_sem=relay_send.at[target_slot, chunk],
            recv_sem=coord_recv.at[target_slot, chunk],
            device_id=at(t, shift),
            device_id_type=MESH,
        )

    @pl.when(t < times - 1)
    def _():
        for chunk in range(CHUNKS):
            first_copy(0, chunk).start()
            first_copy(1, chunk).start()

            if chunk == 0:

                @pl.when(t == 0)
                def _():
                    for kind in range(3):
                        first_belief(kind).start()

        for chunk in range(CHUNKS):
            first_copy(2, chunk).start()

    def forward(dist, pieces):
        right_in, left_in = dist, n - dist
        last = dist + 1 == half
        for chunk in range(CHUNKS):
            relay(right_in, right_in, chunk, 1).wait_recv()
            if chunk < CHUNKS // 2:
                relay(right_in, dist + 1, chunk, 1).start()
            else:

                @pl.when(jnp.logical_not(last))
                def _():
                    relay(right_in, dist + 1, chunk, 1).start()

            relay(left_in, left_in, chunk, 1).wait_recv()
            if chunk >= CHUNKS // 2:
                relay(left_in, n - dist - 1, chunk, n - 1).start()
            else:

                @pl.when(jnp.logical_not(last))
                def _():
                    relay(left_in, n - dist - 1, chunk, n - 1).start()

            if chunk == 0:

                @pl.when(t == 1)
                def _():
                    pass_belief(right_in, right_in, 1).wait_recv()
                    pass_belief(right_in, dist + 1, 1).start()
                    pass_belief(left_in, left_in, 1).wait_recv()

                    @pl.when(jnp.logical_not(last))
                    def _():
                        pass_belief(left_in, n - dist - 1, n - 1).start()

            if chunk < len(pieces):
                pieces[chunk]()

    def arrive(slot):
        for chunk in range(CHUNKS):
            relay(slot, slot, chunk, 1).wait_recv()

    def make_scores(slot):
        x = block[slot]
        hi = x.astype(jnp.bfloat16)
        lo = (x - hi.astype(jnp.float32)).astype(jnp.bfloat16)
        split_x[pl.ds(0, dim)] = hi
        split_x[pl.ds(dim, dim)] = lo
        split_x[pl.ds(2 * dim, dim)] = hi
        split_x[pl.ds(3 * dim, dim)] = lo
        x_sq[slot] = jnp.sum(x * x, axis=0, keepdims=True)
        score[slot] = lax.dot_general(
            split_y[...],
            split_x[...],
            (((1,), (0,)), ((), ())),
            preferred_element_type=jnp.float32,
        )

    tile = 32

    def fold(slot):
        row = LOG2E * (beliefs[slot] - x_sq[slot])

        @pl.loop(0, local // tile, unroll=4)
        def _(step):
            here = pl.ds(pl.multiple_of(step * tile, tile), tile)
            parts = [
                score[slot, here, pl.ds(k, 128)] + row[:, k : k + 128]
                for k in range(0, local, 128)
            ]
            old = top[here]
            new = old
            for part in parts:
                new = jnp.maximum(new, part)
            acc = total[here] * jnp.exp2(old - new)
            for part in parts:
                acc = acc + jnp.exp2(part - new)
            top[here] = new
            total[here] = acc

    def slot_of(step):
        near = (step + 1) // 2
        return jnp.where(step % 2 == 1, near, lax.rem(n - near, n))

    @pl.when(t > 0)
    def _():
        load_own.wait()
        turned = (own[...] * (2.0 * LOG2E)).T
        hi = turned.astype(jnp.bfloat16)
        lo = (turned - hi.astype(jnp.float32)).astype(jnp.bfloat16)
        split_y[:, 0:dim] = hi
        split_y[:, dim : 2 * dim] = hi
        split_y[:, 2 * dim : 3 * dim] = lo
        split_y[:, 3 * dim : 4 * dim] = lo
        top[...] = jnp.full_like(top, -1e30)
        total[...] = jnp.zeros_like(total)

        def first_fold(slot):
            @pl.when(t == 1)
            def _():
                fold(slot)

        def await_belief(slot):
            @pl.when(t == 1)
            def _():
                pass_belief(slot, slot, 1).wait_recv()

        forward(1, ())
        arrive(0)
        await_belief(0)
        make_scores(0)
        first_fold(0)

        @pl.loop(2, half)
        def _(dist):
            right, left = dist - 1, n - dist + 1
            forward(
                dist,
                (
                    lambda: make_scores(right),
                    lambda: first_fold(right),
                    lambda: make_scores(left),
                    lambda: first_fold(left),
                ),
            )

        @pl.loop(n - 3, n)
        def _(step):
            slot = slot_of(step)

            @pl.when(step == n - 1)
            def _():
                arrive(half)
                await_belief(half)

            make_scores(slot)
            first_fold(slot)

        @pl.when(t > 1)
        def _():
            @pl.loop(0, n)
            def _(step):
                slot = slot_of(step)
                belief_copy(sent, slot).wait_recv()
                fold(slot)

        tops = top[...].T
        peak = jnp.max(tops, axis=0, keepdims=True)
        mass = jnp.sum(total[...].T * jnp.exp2(tops - peak), axis=0, keepdims=True)
        load_pot.wait()
        y = own[...]
        y_sq = jnp.sum(y * y, axis=0, keepdims=True)
        sent[...] = (
            LN2 * (peak + jnp.log2(mass)) - y_sq / EPS - math.log(n * local) + pot[...]
        )

        @pl.when(t < times - 1)
        def _():
            @pl.loop(0, n)
            def _(step):
                belief_copy(sent, slot_of(n - 1 - step)).start()

        out_ref[...] = sent[...]

        @pl.loop(1, half)
        def _(dist):
            last = dist + 1 == half

            @pl.when(t == 1)
            def _():
                pass_belief(dist, dist + 1, 1).wait_send()

                @pl.when(jnp.logical_not(last))
                def _():
                    pass_belief(n - dist, n - dist - 1, n - 1).wait_send()

            for chunk in range(CHUNKS):
                if chunk < CHUNKS // 2:
                    relay(dist, dist + 1, chunk, 1).wait_send()
                else:

                    @pl.when(jnp.logical_not(last))
                    def _():
                        relay(dist, dist + 1, chunk, 1).wait_send()

                if chunk >= CHUNKS // 2:
                    relay(n - dist, n - dist - 1, chunk, n - 1).wait_send()
                else:

                    @pl.when(jnp.logical_not(last))
                    def _():
                        relay(n - dist, n - dist - 1, chunk, n - 1).wait_send()

    @pl.when(t == 0)
    def _():
        load_own.wait()
        load_pot.wait()
        for kind in range(3):
            first_belief(kind).wait_send()
        out_ref[...] = pot[...]

    @pl.when(t < times - 1)
    def _():
        for chunk in range(CHUNKS):
            for kind in range(3):
                first_copy(kind, chunk).wait_send()

        @pl.when(t > 0)
        def _():
            @pl.loop(0, n)
            def _(shift):
                belief_copy(sent, shift).wait_send()


def body(n, times, coords, potentials):
    _, dim, local = coords.shape
    f32, bf16 = jnp.float32, jnp.bfloat16
    dma = pltpu.SemaphoreType.DMA
    return pl.pallas_call(
        functools.partial(kernel, n, times),
        out_shape=pltpu.VMEM((1, local), f32),
        in_specs=[pl.BlockSpec(memory_space=pl.ANY)] * 2,
        out_specs=pl.BlockSpec(memory_space=pltpu.VMEM),
        scratch_shapes=[
            pltpu.VMEM((dim, local), f32),
            pltpu.VMEM((1, local), f32),
            pltpu.VMEM((n, dim, local), f32),
            pltpu.VMEM((n, 1, local), f32),
            pltpu.VMEM((1, local), f32),
            pltpu.VMEM((local, 4 * dim), bf16),
            pltpu.VMEM((4 * dim, local), bf16),
            pltpu.VMEM((n, local, local), f32),
            pltpu.VMEM((n, 1, local), f32),
            pltpu.VMEM((local, 128), f32),
            pltpu.VMEM((local, 128), f32),
            dma((2,)),
            dma((3, CHUNKS)),
            dma((n, CHUNKS)),
            dma((n, CHUNKS)),
            dma((n,)),
            dma((n,)),
            dma((n,)),
        ],
        compiler_params=pltpu.CompilerParams(
            collective_id=0, has_side_effects=True, vmem_limit_bytes=60 * 1024 * 1024
        ),
        name="sweep",
    )(coords, potentials)


def solution(mesh):
    return jax.shard_map(
        functools.partial(body, mesh.shape["cell"], mesh.shape["tm"]),
        mesh=mesh,
        in_specs=(P("tm", None, "cell"), P("tm", "cell")),
        out_specs=P("tm", "cell"),
        check_vma=False,
    )
```

```python
import functools
import math

import jax
import jax.numpy as jnp
from jax import lax
from jax.experimental import pallas as pl
from jax.experimental.pallas import tpu as pltpu
from jax.sharding import PartitionSpec as P

EPS = 1.0
LOG2E = math.log2(math.e) / EPS
LN2 = math.log(2.0) * EPS
CHUNKS = 4
MESH = pl.DeviceIdType.MESH


def kernel(
    n,
    times,
    coords_hbm,
    pot_hbm,
    out_ref,
    own,
    pot,
    block,
    beliefs,
    sent,
    split_y,
    split_x,
    score,
    x_sq,
    top,
    total,
    load_sem,
    coord_send,
    relay_send,
    coord_recv,
    belief_send,
    belief_relay,
    belief_recv,
):
    dim, local = own.shape
    half = n // 2
    rows = dim // CHUNKS
    t = lax.axis_index("tm")
    cell = lax.axis_index("cell")
    me = jnp.where(cell % 2 == 0, cell // 2, n - 1 - cell // 2)

    def cell_of(pos):
        return jnp.where(pos < half, 2 * pos, 2 * (n - 1 - pos) + 1)

    def at(group, shift):
        return (group, cell_of(lax.rem(me + shift + n, n)))

    barrier = pltpu.get_barrier_semaphore()

    @pl.when(t > 0)
    def _():
        for shift in (0, 1, n - 1):
            pl.semaphore_signal(barrier, inc=1, device_id=at(t - 1, shift), device_id_type=MESH)
        for shift in (1, n - 1):
            pl.semaphore_signal(barrier, inc=1, device_id=at(t, shift), device_id_type=MESH)

    load_own = pltpu.make_async_copy(coords_hbm.at[0], own, load_sem.at[0])
    load_pot = pltpu.make_async_copy(pot_hbm, pot, load_sem.at[1])
    load_own.start()
    load_pot.start()
    pl.semaphore_wait(barrier, jnp.where(t < times - 1, 3, 0) + jnp.where(t > 0, 2, 0))

    def first_copy(kind, chunk):
        shift = (1, n - 1, 0)[kind]
        return pltpu.make_async_remote_copy(
            src_ref=coords_hbm.at[0, pl.ds(chunk * rows, rows)],
            dst_ref=block.at[shift, pl.ds(chunk * rows, rows)],
            send_sem=coord_send.at[kind, chunk],
            recv_sem=coord_recv.at[shift, chunk],
            device_id=at(t + 1, shift),
            device_id_type=MESH,
        )

    def first_belief(kind):
        shift = (1, n - 1, 0)[kind]
        return pltpu.make_async_remote_copy(
            src_ref=pot_hbm,
            dst_ref=beliefs.at[shift],
            send_sem=belief_send.at[shift],
            recv_sem=belief_recv.at[shift],
            device_id=at(t + 1, shift),
            device_id_type=MESH,
        )

    def pass_belief(source_slot, target_slot, shift):
        return pltpu.make_async_remote_copy(
            src_ref=beliefs.at[source_slot],
            dst_ref=beliefs.at[target_slot],
            send_sem=belief_relay.at[target_slot],
            recv_sem=belief_recv.at[target_slot],
            device_id=at(t, shift),
            device_id_type=MESH,
        )

    def belief_copy(source, shift):
        return pltpu.make_async_remote_copy(
            src_ref=source,
            dst_ref=beliefs.at[shift],
            send_sem=belief_send.at[shift],
            recv_sem=belief_recv.at[shift],
            device_id=at(t + 1, shift),
            device_id_type=MESH,
        )

    def relay(source_slot, target_slot, chunk, shift):
        return pltpu.make_async_remote_copy(
            src_ref=block.at[source_slot, pl.ds(chunk * rows, rows)],
            dst_ref=block.at[target_slot, pl.ds(chunk * rows, rows)],
            send_sem=relay_send.at[target_slot, chunk],
            recv_sem=coord_recv.at[target_slot, chunk],
            device_id=at(t, shift),
            device_id_type=MESH,
        )

    @pl.when(t < times - 1)
    def _():
        for chunk in range(CHUNKS):
            first_copy(0, chunk).start()
            first_copy(1, chunk).start()

            if chunk == 0:

                @pl.when(t == 0)
                def _():
                    for kind in range(3):
                        first_belief(kind).start()

        for chunk in range(CHUNKS):
            first_copy(2, chunk).start()

    def forward(dist, pieces):
        right_in, left_in = dist, n - dist
        last = dist + 1 == half
        for chunk in range(CHUNKS):
            relay(right_in, right_in, chunk, 1).wait_recv()
            if chunk < CHUNKS // 2:
                relay(right_in, dist + 1, chunk, 1).start()
            else:

                @pl.when(jnp.logical_not(last))
                def _():
                    relay(right_in, dist + 1, chunk, 1).start()

            relay(left_in, left_in, chunk, 1).wait_recv()
            if chunk >= CHUNKS // 2:
                relay(left_in, n - dist - 1, chunk, n - 1).start()
            else:

                @pl.when(jnp.logical_not(last))
                def _():
                    relay(left_in, n - dist - 1, chunk, n - 1).start()

            if chunk == 0:

                @pl.when(t == 1)
                def _():
                    pass_belief(right_in, right_in, 1).wait_recv()
                    pass_belief(right_in, dist + 1, 1).start()
                    pass_belief(left_in, left_in, 1).wait_recv()

                    @pl.when(jnp.logical_not(last))
                    def _():
                        pass_belief(left_in, n - dist - 1, n - 1).start()

            if chunk < len(pieces):
                pieces[chunk]()

    def arrive(slot):
        for chunk in range(CHUNKS):
            relay(slot, slot, chunk, 1).wait_recv()

    def make_scores(slot):
        x = block[slot]
        hi = x.astype(jnp.bfloat16)
        lo = (x - hi.astype(jnp.float32)).astype(jnp.bfloat16)
        split_x[pl.ds(0, dim)] = hi
        split_x[pl.ds(dim, dim)] = lo
        split_x[pl.ds(2 * dim, dim)] = hi
        split_x[pl.ds(3 * dim, dim)] = lo
        x_sq[slot] = jnp.sum(x * x, axis=0, keepdims=True)
        score[slot] = lax.dot_general(
            split_y[...],
            split_x[...],
            (((1,), (0,)), ((), ())),
            preferred_element_type=jnp.float32,
        )

    tile = 32

    def fold(*slots):
        rows_of = [LOG2E * (beliefs[slot] - x_sq[slot]) for slot in slots]
        size = tile // len(slots)

        @pl.loop(0, local // size, unroll=4)
        def _(step):
            here = pl.ds(pl.multiple_of(step * size, size), size)
            parts = [
                score[slot, here, pl.ds(k, 128)] + row[:, k : k + 128]
                for slot, row in zip(slots, rows_of)
                for k in range(0, local, 128)
            ]
            old = top[here]
            new = old
            for part in parts:
                new = jnp.maximum(new, part)
            acc = total[here] * jnp.exp2(old - new)
            for part in parts:
                acc = acc + jnp.exp2(part - new)
            top[here] = new
            total[here] = acc

    def slot_of(step):
        near = (step + 1) // 2
        return jnp.where(step % 2 == 1, near, lax.rem(n - near, n))

    @pl.when(t > 0)
    def _():
        load_own.wait()
        turned = (own[...] * (2.0 * LOG2E)).T
        hi = turned.astype(jnp.bfloat16)
        lo = (turned - hi.astype(jnp.float32)).astype(jnp.bfloat16)
        split_y[:, 0:dim] = hi
        split_y[:, dim : 2 * dim] = hi
        split_y[:, 2 * dim : 3 * dim] = lo
        split_y[:, 3 * dim : 4 * dim] = lo
        top[...] = jnp.full_like(top, -1e30)
        total[...] = jnp.zeros_like(total)

        def first_fold(slot):
            @pl.when(t == 1)
            def _():
                fold(slot)

        def await_belief(slot):
            @pl.when(t == 1)
            def _():
                pass_belief(slot, slot, 1).wait_recv()

        forward(1, ())
        arrive(0)
        await_belief(0)
        make_scores(0)
        first_fold(0)

        @pl.loop(2, half)
        def _(dist):
            right, left = dist - 1, n - dist + 1
            forward(
                dist,
                (
                    lambda: make_scores(right),
                    lambda: first_fold(right),
                    lambda: make_scores(left),
                    lambda: first_fold(left),
                ),
            )

        @pl.loop(n - 3, n)
        def _(step):
            slot = slot_of(step)

            @pl.when(step == n - 1)
            def _():
                arrive(half)
                await_belief(half)

            make_scores(slot)
            first_fold(slot)

        @pl.when(t > 1)
        def _():
            belief_copy(sent, 0).wait_recv()
            fold(0)

            @pl.loop(1, half)
            def _(dist):
                belief_copy(sent, dist).wait_recv()
                belief_copy(sent, n - dist).wait_recv()
                fold(dist, n - dist)

            belief_copy(sent, half).wait_recv()
            fold(half)

        tops = top[...].T
        peak = jnp.max(tops, axis=0, keepdims=True)
        mass = jnp.sum(total[...].T * jnp.exp2(tops - peak), axis=0, keepdims=True)
        load_pot.wait()
        y = own[...]
        y_sq = jnp.sum(y * y, axis=0, keepdims=True)
        sent[...] = (
            LN2 * (peak + jnp.log2(mass)) - y_sq / EPS - math.log(n * local) + pot[...]
        )

        @pl.when(t < times - 1)
        def _():
            @pl.loop(0, n)
            def _(step):
                belief_copy(sent, slot_of(n - 1 - step)).start()

        out_ref[...] = sent[...]

        @pl.loop(1, half)
        def _(dist):
            last = dist + 1 == half

            @pl.when(t == 1)
            def _():
                pass_belief(dist, dist + 1, 1).wait_send()

                @pl.when(jnp.logical_not(last))
                def _():
                    pass_belief(n - dist, n - dist - 1, n - 1).wait_send()

            for chunk in range(CHUNKS):
                if chunk < CHUNKS // 2:
                    relay(dist, dist + 1, chunk, 1).wait_send()
                else:

                    @pl.when(jnp.logical_not(last))
                    def _():
                        relay(dist, dist + 1, chunk, 1).wait_send()

                if chunk >= CHUNKS // 2:
                    relay(n - dist, n - dist - 1, chunk, n - 1).wait_send()
                else:

                    @pl.when(jnp.logical_not(last))
                    def _():
                        relay(n - dist, n - dist - 1, chunk, n - 1).wait_send()

    @pl.when(t == 0)
    def _():
        load_own.wait()
        load_pot.wait()
        for kind in range(3):
            first_belief(kind).wait_send()
        out_ref[...] = pot[...]

    @pl.when(t < times - 1)
    def _():
        for chunk in range(CHUNKS):
            for kind in range(3):
                first_copy(kind, chunk).wait_send()

        @pl.when(t > 0)
        def _():
            @pl.loop(0, n)
            def _(shift):
                belief_copy(sent, shift).wait_send()


def body(n, times, coords, potentials):
    _, dim, local = coords.shape
    f32, bf16 = jnp.float32, jnp.bfloat16
    dma = pltpu.SemaphoreType.DMA
    return pl.pallas_call(
        functools.partial(kernel, n, times),
        out_shape=pltpu.VMEM((1, local), f32),
        in_specs=[pl.BlockSpec(memory_space=pl.ANY)] * 2,
        out_specs=pl.BlockSpec(memory_space=pltpu.VMEM),
        scratch_shapes=[
            pltpu.VMEM((dim, local), f32),
            pltpu.VMEM((1, local), f32),
            pltpu.VMEM((n, dim, local), f32),
            pltpu.VMEM((n, 1, local), f32),
            pltpu.VMEM((1, local), f32),
            pltpu.VMEM((local, 4 * dim), bf16),
            pltpu.VMEM((4 * dim, local), bf16),
            pltpu.VMEM((n, local, local), f32),
            pltpu.VMEM((n, 1, local), f32),
            pltpu.VMEM((local, 128), f32),
            pltpu.VMEM((local, 128), f32),
            dma((2,)),
            dma((3, CHUNKS)),
            dma((n, CHUNKS)),
            dma((n, CHUNKS)),
            dma((n,)),
            dma((n,)),
            dma((n,)),
        ],
        compiler_params=pltpu.CompilerParams(
            collective_id=0, has_side_effects=True, vmem_limit_bytes=60 * 1024 * 1024
        ),
        name="sweep",
    )(coords, potentials)


def solution(mesh):
    return jax.shard_map(
        functools.partial(body, mesh.shape["cell"], mesh.shape["tm"]),
        mesh=mesh,
        in_specs=(P("tm", None, "cell"), P("tm", "cell")),
        out_specs=P("tm", "cell"),
        check_vma=False,
    )
```
